32 devices in a mesh: rep: 2 (over x), exp: 16 (over z, y, core).
Axes of the slice: x: 2, y: 2, z: 4, core: 2. Of those that a mesh axis runs over, the one named last changes fastest.
Arguments:
- hidden: bfloat16 [2, 16, 320, 768], P('rep', 'exp'), may hold values from -6 to 6
- down_weight: bfloat16 [16, 768, 4096], P('exp', None, 'rep'), may hold values from -0.21875 to 0.21875
- grad_out: bfloat16 [4096, 4096], P(('rep', 'exp')), may hold values from -6 to 6
- expert_ids: int32 [4096, 2], P(('rep', 'exp')), may hold values from 0 to 15, all different within a row; in each aligned block of 128 rows (0 to 127, 128 to 255, ...) at most 20 rows name the same one
- gate_weights: float32 [4096, 2], P(('rep', 'exp')), may hold values from 0.03 to 0.4
Outputs:
- combined: bfloat16 [4096, 4096], P(('rep', 'exp'))
- hidden_grad: bfloat16 [2, 16, 320, 768], P('rep', 'exp')
- weight_grad: bfloat16 [16, 768, 4096], P('exp', None, 'rep')
- gate_grad: float32 [4096, 2], P(('rep', 'exp'))
The draws below stay inside these ranges and needn't reach their ends.
Inputs may be any that keep to these rules, and one draw needn't show every extreme that they name: `expert_ids`: A token names 2 different experts. Within the 128 tokens of one device no expert is named more than 20 times, a bound that some block reaches.
All inputs are finite; a program needn't handle non-finite values.
Results may differ from the reference program's by a relative error of at most 0.014.
Values may be sent and summed in bfloat16 or wider, within the bound.
No kernel may reach another device: no remote copies, remote signals or barrier semaphores. Data moves between devices by JAX's collectives and lax.ppermute only.
A program may use at most 64 MiB of HBM per device.

```python
import math
import jax
import jax.numpy as jnp
import numpy as np
from jax import lax

D = 4096
FF = 768
TOP = 2
TOK_DEV = 128
EXPERTS = 16
CAP = 20
TOKENS = 4096
N_REP = 2
N_EXP = 16


def block_levels(own_key, extent, split, least, high):
    gain, own = 1.0, jax.random.fold_in(own_key, 6)
    for dim, blocks in split:
        heights = jnp.exp(jax.random.uniform(jax.random.fold_in(own, dim), (blocks,), jnp.float32, least / len(split), high / len(split)))
        gain = gain * jnp.repeat(heights, extent[dim] // blocks).reshape([-1 if axis == dim else 1 for axis in range(len(extent))])
    return gain


def deal_out(key, own, number, rows, number_of, top, bound, lean):
    order = jax.random.permutation(key, number_of)
    packed, ordinary = shares(number_of, rows * top, bound, lean, True), shares(number_of, rows * top, bound, lean, False)
    places = jnp.arange(number_of)

    def named(lengths, turn):
        used = int((lengths > 0).sum())
        fixed = max(1, used // 4)
        shifted = fixed + (places - fixed + turn * (used - fixed)) % max(1, number_of - fixed)
        return jnp.zeros((number_of,), jnp.int32).at[order[jnp.where(places < fixed, places, shifted)]].set(jnp.asarray(lengths, jnp.int32))

    lengths = jnp.where(number % 4 == 0, named(packed, number // 4), named(ordinary, number - number // 4 - 1))
    mixed = jax.random.permutation(jax.random.fold_in(own, 3), number_of)
    donor, taker = mixed[0:number_of // 2 * 2:2], mixed[1:number_of // 2 * 2:2]
    room = jnp.minimum(lengths[donor] - 1, bound - lengths[taker]) // 2
    room = jnp.where((donor == order[0]) | (taker == order[0]) | (lengths[taker] == 0), 0, jnp.maximum(room, 0))
    shifted = jax.random.randint(jax.random.fold_in(own, 4), (number_of // 2,), 0, 1 << 20) % (room + 1)
    lengths = lengths.at[donor].add(-shifted).at[taker].add(shifted)
    labels = jnp.searchsorted(jnp.cumsum(lengths), jnp.arange(rows * top), side="right").astype(jnp.int32)
    listing = labels.reshape(top, rows).T
    listing = listing[jax.random.permutation(jax.random.fold_in(own, 1), rows)]
    turn = jax.random.randint(jax.random.fold_in(own, 2), (rows, 1), 0, top)
    return jnp.take_along_axis(listing, (jnp.arange(top)[None, :] + turn) % top, axis=1)


def shares(number_of, total, most, lean, full):
    loads = [(1 << 20) // math.isqrt(rank ** lean) + 1 for rank in range(1, number_of + 1)]
    largest = most if full else min(most, max(-(-total // number_of), total * loads[0] // sum(loads)))
    least = 1 if total - largest >= number_of - 1 else 0
    holding, spare = [largest] + [least] * (number_of - 1), total - largest - least * (number_of - 1)
    while spare > 0:
        free = [i for i in range(1, number_of) if holding[i] < largest] or [i for i in range(1, number_of) if holding[i] < most]
        pool, left = sum([loads[i] for i in free]), spare
        for i in free:
            addition = min(most - holding[i], max(1, left * loads[i] // pool), spare)
            holding[i] = holding[i] + addition
            spare = spare - addition
    return np.array(holding)


def bell_draw(stream_key, dims, spread, reach, cuts=(), held_as=jnp.bfloat16):
    entries = spread * jax.random.normal(stream_key, dims, jnp.float32)
    if cuts:
        entries = entries * block_levels(stream_key, dims, cuts, -0.22, 0.18)
    return jnp.clip(entries, -reach, reach).astype(held_as)


def setup_inputs(seed: int = 0) -> dict:
    key_list = jax.random.split(jax.random.key(seed), 6)
    hidden = bell_draw(key_list[0], (N_REP, EXPERTS, N_EXP * CAP, FF), 1.0, 6.0, ((0, 2), (1, 16)))
    down_weight = bell_draw(key_list[1], (EXPERTS, FF, D), FF ** -0.5, 0.21875, ((0, 16), (2, 2)))
    grad_out = bell_draw(key_list[2], (TOKENS, D), 1.0, 6.0, ((0, 32),))
    expert_ids_keys = jax.random.split(jax.random.fold_in(key_list[3], 1), TOKENS // TOK_DEV)
    expert_ids_turns = jax.random.permutation(jax.random.fold_in(key_list[3], 3), TOKENS // TOK_DEV)
    expert_ids = jax.vmap(lambda own, number: deal_out(jax.random.fold_in(key_list[3], 2), own, number, TOK_DEV, EXPERTS, TOP, CAP, 2))(expert_ids_keys, expert_ids_turns).reshape((TOKENS, TOP))
    gate_weights = jnp.clip(jnp.exp(math.log(0.4) - 2.5902672 * jax.random.uniform(key_list[4], (TOKENS, TOP), jnp.float32) ** block_levels(key_list[4], (TOKENS, TOP), ((0, 32),), -0.2, 0.2)), 0.03, 0.4)
    return dict(hidden=hidden, down_weight=down_weight, grad_out=grad_out, expert_ids=expert_ids, gate_weights=gate_weights)


def reference(hidden, down_weight, grad_out, expert_ids, gate_weights):
    slots_all = N_EXP * CAP
    slice_width = D // N_REP
    routed = expert_ids.reshape(N_REP, N_EXP, TOK_DEV, TOP)
    matches = (routed[..., None] == jnp.arange(EXPERTS, dtype=jnp.int32)).astype(jnp.int32)
    per_token = jnp.sum(matches, axis=3).astype(jnp.int32)
    before = (jnp.cumsum(per_token, axis=2) - per_token).astype(jnp.int32)
    position = jnp.sum(matches * before[:, :, :, None, :], axis=4).astype(jnp.int32)
    slot_index = (jnp.arange(N_EXP, dtype=jnp.int32)[None, :, None, None] * CAP + position).astype(jnp.int32)
    replica = jnp.broadcast_to(jnp.arange(N_REP, dtype=jnp.int32)[:, None, None, None], routed.shape)
    token_index = jnp.broadcast_to(jnp.arange(TOKENS, dtype=jnp.int32).reshape(N_REP, N_EXP, TOK_DEV, 1), routed.shape)
    token_table = jnp.zeros((N_REP, EXPERTS, slots_all), jnp.int32).at[replica, routed, slot_index].set(token_index)
    gate_table = jnp.zeros((N_REP, EXPERTS, slots_all), jnp.float32).at[replica, routed, slot_index].set(gate_weights.reshape(routed.shape))

    def one_expert(mixed_sum, inputs):
        slot_rows, weight, tokens, slot_gates = inputs
        expert_out = jnp.einsum("rnf,fd->rnd", slot_rows.astype(jnp.float32), weight.astype(jnp.float32)).astype(jnp.bfloat16)
        out_wide = expert_out.astype(jnp.float32)
        flat_tokens = tokens.reshape(-1)
        mixed_sum = mixed_sum.at[flat_tokens].add((slot_gates[..., None] * out_wide).reshape(-1, D))
        upstream = grad_out[tokens].astype(jnp.float32)
        scores = jnp.sum(upstream * out_wide, axis=2)
        slot_grad = (upstream * slot_gates[..., None]).astype(jnp.bfloat16)
        weight_part = jnp.einsum("rnf,rnd->fd", slot_rows.astype(jnp.float32), slot_grad.astype(jnp.float32)).astype(jnp.bfloat16)
        pieces = jnp.einsum("rnqd,fqd->rnqf", slot_grad.astype(jnp.float32).reshape(N_REP, slots_all, N_REP, slice_width), weight.astype(jnp.float32).reshape(FF, N_REP, slice_width)).astype(jnp.bfloat16)
        hidden_part = jnp.sum(pieces.astype(jnp.float32), axis=2).astype(jnp.bfloat16)
        return mixed_sum, (weight_part, hidden_part, scores)

    start_sum = jnp.zeros((TOKENS, D), jnp.float32)
    inputs = (jnp.swapaxes(hidden, 0, 1), down_weight, jnp.swapaxes(token_table, 0, 1), jnp.swapaxes(gate_table, 0, 1))
    mixed_sum, (weight_grad, hidden_parts, scores) = lax.scan(one_expert, start_sum, inputs)
    hidden_grad = jnp.swapaxes(hidden_parts, 0, 1)
    gate_grad = scores[routed, replica, slot_index].reshape(TOKENS, TOP)
    return (mixed_sum.astype(jnp.bfloat16), hidden_grad, weight_grad, gate_grad)
```

```python
import functools

import jax
import jax.numpy as jnp
from jax import lax
from jax.experimental import pallas as pl
from jax.experimental.pallas import tpu as pltpu
from jax.sharding import PartitionSpec as P


PLANES = 4
SEATS = 4
BF16 = jnp.bfloat16
F32 = jnp.float32


def slot_tables(routed, gate_weights, expert_count, capacity):
    token_count = routed.shape[0]
    matches = (routed[:, :, None] == jnp.arange(expert_count, dtype=jnp.int32)).astype(jnp.int32)
    per_token = jnp.sum(matches, axis=1)
    before = jnp.cumsum(per_token, axis=0) - per_token
    position = jnp.sum(matches * before[:, None, :], axis=2)
    target = routed * capacity + position
    matched = target[:, :, None] == jnp.arange(expert_count * capacity, dtype=jnp.int32)
    token_index = jnp.arange(token_count, dtype=jnp.int32)[:, None, None]
    slot_token = jnp.sum(jnp.where(matched, token_index, 0), axis=(0, 1))
    slot_gate = jnp.sum(jnp.where(matched, gate_weights[:, :, None], 0.0), axis=(0, 1))
    return (target, slot_token, slot_gate)


def general(hidden, down_weight, grad_out, expert_ids, gate_weights):
    rep_count = lax.axis_size("rep")
    exp_count = lax.axis_size("exp")
    slots_all = hidden.shape[2]
    capacity = slots_all // exp_count
    token_count, model_width = grad_out.shape
    top_count = expert_ids.shape[1]
    slice_width = model_width // rep_count
    target, slot_token, slot_gate = slot_tables(expert_ids, gate_weights, exp_count, capacity)
    weights_local = down_weight[0]
    grad_split = (
        grad_out.reshape(token_count, rep_count, slice_width).transpose(1, 0, 2).astype(F32)
    )
    outgoing = (jnp.take(grad_split, slot_token, axis=1) * slot_gate[None, :, None]).astype(BF16)
    outgoing = outgoing.reshape(rep_count, exp_count, capacity, slice_width)
    arrived = lax.all_to_all(
        lax.all_to_all(outgoing, "exp", split_axis=1, concat_axis=1, tiled=True),
        "rep",
        split_axis=0,
        concat_axis=0,
        tiled=True,
    )
    arrived = arrived.reshape(rep_count, slots_all, slice_width)
    gathered = lax.all_gather(hidden[0], "rep", axis=0, tiled=True)
    outputs = jnp.einsum(
        "rnf,fd->rnd", gathered, weights_local, preferred_element_type=F32
    ).astype(BF16)
    outputs = outputs.reshape(rep_count, exp_count, capacity, slice_width)
    returned = lax.all_to_all(
        lax.all_to_all(outputs, "exp", split_axis=1, concat_axis=1, tiled=True),
        "rep",
        split_axis=0,
        concat_axis=0,
        tiled=True,
    )
    returned = returned.reshape(rep_count, exp_count * capacity, slice_width)
    weight_grad = jnp.einsum(
        "rnf,rnd->fd", gathered, arrived, preferred_element_type=F32
    ).astype(BF16)[None]
    hidden_sum = lax.psum_scatter(
        jnp.einsum(
            "rnd,fd->rnf", arrived, weights_local, preferred_element_type=F32
        ).astype(BF16),
        "rep",
        scatter_dimension=0,
        tiled=True,
    )
    picked = jnp.take(returned, target.reshape(-1), axis=1)
    picked = picked.reshape(rep_count, token_count, top_count, slice_width).transpose(1, 2, 0, 3)
    picked = picked.reshape(token_count, top_count, model_width).astype(F32)
    combined = jnp.sum(gate_weights[:, :, None] * picked, axis=1).astype(BF16)
    gate_grad = jnp.sum(grad_out.astype(F32)[:, None, :] * picked, axis=2)
    return (combined, hidden_sum[None], weight_grad, gate_grad)


def part(index, unit, count):
    return sum([(index >= unit * i).astype(jnp.int32) for i in range(1, count)])


def axes(shape, dim, capacity):
    row = lax.broadcasted_iota(jnp.int32, shape, dim)
    width = PLANES * capacity
    j = part(row, width, SEATS)
    rest = row - j * width
    g = part(rest, capacity, PLANES)
    return j, g, rest - g * capacity


def hot(mask):
    return jnp.where(mask, 1.0, 0.0).astype(BF16)


def names(table, wanted):
    wanted = wanted.astype(F32)
    return wanted == table[0:1, :], wanted == table[1:2, :]


def weights_of(table, wanted, keep=None):
    first, second = names(table, wanted)
    if keep is not None:
        first, second = first & keep, second & keep
    return jnp.where(first, table[2:3, :], 0.0) + jnp.where(second, table[3:4, :], 0.0)


def mm(a, b):
    return jnp.dot(a, b, preferred_element_type=F32)


def mm_tn(a, b):
    return lax.dot_general(a, b, (((0,), (0,)), ((), ())), preferred_element_type=F32)


def mm_nt(a, b):
    return lax.dot_general(a, b, (((1,), (1,)), ((), ())), preferred_element_type=F32)


def split_hi_lo(x):
    hi = x.astype(BF16)
    return hi, (x - hi.astype(F32)).astype(BF16)


def start_kernel(cap, place, ids, gates, hidden, table, turned):
    experts, tokens = PLANES * SEATS, ids.shape[1]
    expert = lax.broadcasted_iota(jnp.int32, (experts, tokens), 0)
    first, second = expert == ids[0:1, :], expert == ids[1:2, :]
    earlier = lax.broadcasted_iota(jnp.int32, (tokens, tokens), 0) < lax.broadcasted_iota(
        jnp.int32, (tokens, tokens), 1
    )
    before = mm(hot(first | second), hot(earlier))
    slot = expert.astype(F32) * cap + before
    table[...] = jnp.zeros_like(table)
    table[0:1, :] = jnp.sum(jnp.where(first, slot, 0.0), axis=0, keepdims=True)
    table[1:2, :] = jnp.sum(jnp.where(second, slot, 0.0), axis=0, keepdims=True)
    table[2:4, :] = gates[...]
    rows = hidden.shape[0]
    turned[...] = mm(turn_matrix(place, rows, cap), hidden[...]).astype(BF16)


def turn_matrix(place, rows, cap):
    j, g, slot = axes((rows, rows), 0, cap)
    column = lax.broadcasted_iota(jnp.int32, (rows, rows), 1)
    return hot(column == ((place[0] ^ g) * SEATS + (place[1] ^ j)) * cap + slot)


def out_kernel(turned, weight, *outs):
    full = mm(turned[...], weight[...]).astype(BF16)
    height = outs[0].shape[0]
    for j, out in enumerate(outs):
        out[...] = full[j * height : (j + 1) * height, :]


def near_kernel(cap, place, table, raw, out):
    rows, tokens = out.shape[0], raw.shape[0]
    wanted = (place[0] ^ 1) * rows + lax.broadcasted_iota(jnp.int32, (rows, tokens), 0)
    first, second = names(table[...], wanted)
    out[...] = mm(hot(first | second), raw[...]).astype(BF16)


def relay_kernel(cap, place, line, far_a, far_b, out):
    rows, tokens = out.shape[0] // 2, far_a.shape[0]
    wanted = (place[0] ^ 1) * rows + lax.broadcasted_iota(jnp.int32, (rows, tokens), 0)
    for half, (g, far) in enumerate(((3, far_b), (2, far_a))):
        first, second = names(line[g], wanted)
        out[half * rows : (half + 1) * rows, :] = mm(hot(first | second), far[...]).astype(BF16)


def spread_kernel(cap, place, line, raw, near, far_a, far_b, passed, *rest):
    outs, (m_raw, m_near, m_a, m_b, m_passed, scale) = rest[:SEATS], rest[SEATS:]
    height, tokens = outs[0].shape[0], raw.shape[0]
    rows = SEATS * height

    @pl.when(pl.program_id(0) == 0)
    def _():
        j, g, slot = axes((rows, tokens), 0, cap)
        wanted = place[0] * height + (place[1] ^ j) * cap + slot
        total = jnp.zeros((rows, tokens), F32)
        for group, matrix in ((0, m_raw), (1, None), (2, m_a), (3, m_b)):
            first, second = names(line[group], wanted)
            first, second = first & (g == group), second & (g == group)
            if matrix is not None:
                matrix[...] = hot(first | second)
            total += jnp.where(first, line[group][2:3, :], 0.0)
            total += jnp.where(second, line[group][3:4, :], 0.0)
        scale[...] = jnp.broadcast_to(jnp.sum(total, axis=1, keepdims=True), scale.shape)
        j, g, slot = axes((rows, height), 0, cap)
        column = lax.broadcasted_iota(jnp.int32, (rows, height), 1)
        m_near[...] = hot((g == 1) & (column == (place[1] ^ j) * cap + slot))
        j, g, slot = axes((rows, 2 * height), 0, cap)
        column = lax.broadcasted_iota(jnp.int32, (rows, 2 * height), 1)
        m_passed[...] = hot((g >= 2) & (column == (g - 2) * height + (place[1] ^ j) * cap + slot))

    full = mm(m_raw[...], raw[...]) + mm(m_near[...], near[...])
    full += mm(m_a[...], far_a[...]) + mm(m_b[...], far_b[...]) + mm(m_passed[...], passed[...])
    full = (full * scale[:, 0:1]).astype(BF16)
    for j, out in enumerate(outs):
        out[...] = full[j * height : (j + 1) * height, :]


def expert_kernel(cap, place, weight, turned, a0, a1, a2, a3, partial, scores, total):
    arrived = jnp.concatenate([a0[...], a1[...], a2[...], a3[...]], axis=0)
    step = pl.program_id(0)

    @pl.when(step == 0)
    def _():
        total[...] = jnp.zeros_like(total)

    total[...] += mm_nt(arrived, weight[...])

    @pl.when(step == pl.num_programs(0) - 1)
    def _():
        whole = total[...]
        partial[...] = whole.astype(BF16)
        score = jnp.sum(whole * turned[...].astype(F32), axis=1, keepdims=True)
        rows, lanes = whole.shape[0], scores.shape[1]
        j, g, slot = axes((rows, lanes), 0, cap)
        column = lax.broadcasted_iota(jnp.int32, (rows, lanes), 1)
        spread = jnp.where(column == slot, score, 0.0)
        sources = scores.shape[0]
        j, g, slot = axes((sources, rows), 1, cap)
        source = lax.broadcasted_iota(jnp.int32, (sources, rows), 0)
        pick = jnp.where(source == (place[0] ^ g) * SEATS + (place[1] ^ j), 1.0, 0.0)
        scores[...] = jnp.dot(
            pick, spread, preferred_element_type=F32, precision=lax.Precision.HIGHEST
        )


def weight_kernel(own_turned, other_turned, *rest):
    own, other, out = rest[:SEATS], rest[SEATS : 2 * SEATS], rest[2 * SEATS]
    first = jnp.concatenate([r[...] for r in own], axis=0)
    second = jnp.concatenate([r[...] for r in other], axis=0)
    out[...] = (mm_tn(own_turned[...], first) + mm_tn(other_turned[...], second)).astype(BF16)


def hidden_kernel(cap, place, mine, theirs, out):
    total = (mine[...].astype(F32) + theirs[...].astype(F32)).astype(BF16)
    out[...] = mm_tn(turn_matrix(place, total.shape[0], cap), total).astype(BF16)


def sort_kernel(cap, q0, q1, q2, q3, near, passed):
    full = jnp.concatenate([q0[...], q1[...], q2[...], q3[...]], axis=0)
    height, rows = near.shape[0], full.shape[0]
    j, g, slot = axes((3 * height, rows), 1, cap)
    row = lax.broadcasted_iota(jnp.int32, (3 * height, rows), 0)
    chosen = hot((g >= 1) & (row == (g - 1) * height + j * cap + slot))
    out = mm(chosen, full).astype(BF16)
    near[...] = out[:height, :]
    passed[...] = out[height:, :]


def blend(weights, rows):
    hi, lo = split_hi_lo(weights)
    return mm_tn(hi, rows) + mm_tn(lo, rows)


def merge_kernel(cap, place, line, q0, q1, q2, q3, passed, to_a, to_b):
    full = jnp.concatenate([q0[...], q1[...], q2[...], q3[...]], axis=0)
    more = passed[...]
    rows, height, tokens = full.shape[0], q0.shape[0], to_a.shape[0]
    j, g, slot = axes((rows, tokens), 0, cap)
    wanted = place[0] * height + (place[1] ^ j) * cap + slot
    row = lax.broadcasted_iota(jnp.int32, (2 * height, tokens), 0)
    half = part(row, height, 2)
    rest = row - half * height
    seat = part(rest, cap, SEATS)
    beyond = (place[0] ^ 1) * height + (place[1] ^ seat) * cap + rest - seat * cap
    for group, out in ((2, to_a), (3, to_b)):
        near = blend(weights_of(line[group], wanted, g == group), full)
        far = blend(weights_of(line[group], beyond, half == 3 - group), more)
        out[...] = (near + far).astype(BF16)


def token_rows(cap, place, table, q, near, dense_a, dense_b):
    full = jnp.concatenate([r[...] for r in q], axis=0)
    rows, height, tokens = full.shape[0], q[0].shape[0], dense_a.shape[0]
    j, g, slot = axes((rows, tokens), 0, cap)
    wanted = place[0] * height + (place[1] ^ j) * cap + slot
    total = blend(weights_of(table, wanted, g == 0), full)
    row = lax.broadcasted_iota(jnp.int32, (height, tokens), 0)
    seat = part(row, cap, SEATS)
    beyond = (place[0] ^ 1) * height + (place[1] ^ seat) * cap + row - seat * cap
    total += blend(weights_of(table, beyond), near[...])
    return total + dense_a[...].astype(F32) + dense_b[...].astype(F32)


def other_tokens_kernel(cap, place, line, q0, q1, q2, q3, near, dense_a, dense_b, out):
    out[...] = token_rows(cap, place, line[0], (q0, q1, q2, q3), near, dense_a, dense_b).astype(BF16)


def own_tokens_kernel(
    cap, place, line, ids, scores, crossed, q0, q1, q2, q3, near, dense_a, dense_b, out, gate_grad
):
    width = crossed.shape[1]
    table = line[0]
    mine = token_rows(cap, place, table, (q0, q1, q2, q3), near, dense_a, dense_b).astype(BF16)
    out[:, pl.ds(pl.multiple_of(place[2] * width, width), width)] = mine
    out[:, pl.ds(pl.multiple_of((1 - place[2]) * width, width), width)] = crossed[...]
    sources, lanes = scores.shape
    tokens = mine.shape[0]
    expert = lax.broadcasted_iota(jnp.int32, (sources, tokens), 0)
    lane = lax.broadcasted_iota(jnp.int32, (lanes, tokens), 0).astype(F32)
    for k in range(2):
        name = ids[k : k + 1, :]
        chosen = jnp.where(expert == name, 1.0, 0.0)
        spread = lax.dot_general(
            scores[...],
            chosen,
            (((0,), (0,)), ((), ())),
            preferred_element_type=F32,
            precision=lax.Precision.HIGHEST,
        )
        position = table[k : k + 1, :] - name.astype(F32) * cap
        score = jnp.sum(jnp.where(lane == position, spread, 0.0), axis=0, keepdims=True)
        gate_grad[k : k + 1, :] = score / table[2 + k : 3 + k, :]


SMEM = pl.BlockSpec(memory_space=pltpu.SMEM)


def call(kernel, outs, args, name, blocked=None, tile=None, out_blocked=None, scratch=(), flops=0):
    shapes = [jax.ShapeDtypeStruct(s, d) for s, d in outs]
    moved = sum(a.size * a.dtype.itemsize for a in args) + sum(
        s.size * s.dtype.itemsize for s in shapes
    )
    blocked = blocked or [False] * len(args)
    out_blocked = out_blocked or [False] * len(outs)

    def spec(shape, cut):
        if cut:
            return pl.BlockSpec((shape[0], tile), lambda i: (0, i))
        return pl.BlockSpec(shape, lambda *i: (0,) * len(shape))

    grid = ()
    if tile:
        width = next(a.shape[1] for a, cut in zip(args, blocked) if cut)
        grid = (width // tile,)
    in_specs = [
        SMEM if (a.ndim == 1 and a.dtype == jnp.int32) else spec(a.shape, cut)
        for a, cut in zip(args, blocked)
    ]
    return pl.pallas_call(
        kernel,
        out_shape=shapes,
        grid=grid,
        in_specs=in_specs,
        out_specs=[spec(s.shape, cut) for s, cut in zip(shapes, out_blocked)],
        scratch_shapes=list(scratch),
        compiler_params=pltpu.CompilerParams(vmem_limit_bytes=48 << 20),
        cost_estimate=pl.CostEstimate(flops=int(flops), bytes_accessed=int(moved), transcendentals=0),
        name=name,
    )(*args)


def over_planes(moves):
    return [
        (a * SEATS + seat, b * SEATS + seat) for a, b in moves for seat in range(SEATS)
    ]


FAR_A = over_planes([(0, 2), (3, 1)])
FAR_B = over_planes([(1, 2), (2, 1)])
OUTWARD = over_planes([(2, 3), (1, 0)])
INWARD = over_planes([(3, 2), (0, 1)])
BACK_A = over_planes([(2, 0), (1, 3)])
BACK_B = over_planes([(2, 1), (1, 2)])


def send(x, pairs):
    return lax.ppermute(x, "exp", pairs)


def swap(x):
    return lax.ppermute(x, "rep", [(0, 1), (1, 0)])


def flip(x, bits):
    return send(x, [(s, s ^ bits) for s in range(PLANES * SEATS)])


def planes_and_seats(hidden, down_weight, grad_out, expert_ids, gate_weights):
    replica, device = lax.axis_index("rep"), lax.axis_index("exp")
    place = jnp.stack([device // SEATS, device % SEATS, replica]).astype(jnp.int32)
    rows, depth = hidden.shape[2:]
    experts = PLANES * SEATS
    cap = rows // experts
    height = PLANES * cap
    tokens, width = grad_out.shape[0], grad_out.shape[1] // 2
    weight = down_weight[0]
    tile = width // 2 if width % 512 == 0 else width
    ids, gates = expert_ids.T, gate_weights.T
    bind = functools.partial

    table, turned_own = call(
        bind(start_kernel, cap),
        [((8, tokens), F32), ((rows, depth), BF16)],
        [place, ids, gates, hidden[0, 0]],
        "tables",
    )
    raw_own = lax.dynamic_slice_in_dim(grad_out, replica * width, width, axis=1)
    raw_leaving = lax.dynamic_slice_in_dim(grad_out, (1 - replica) * width, width, axis=1)
    far_own = send(raw_own, FAR_A), send(raw_own, FAR_B)
    turned_other = swap(turned_own)
    raw_other = swap(raw_leaving)
    line_own = jnp.stack([table] + [flip(table, g * SEATS) for g in range(1, PLANES)])
    line_other = swap(line_own)

    def outputs(turned):
        blocks = call(
            out_kernel,
            [((height, width), BF16)] * SEATS,
            [turned, weight],
            "project",
            [False, True],
            tile,
            [True] * SEATS,
            flops=2 * rows * depth * width,
        )
        return [blocks[0]] + [flip(blocks[j], j) for j in range(1, SEATS)]

    def near_rows(line_first, raw):
        payload = call(
            bind(near_kernel, cap),
            [((height, width), BF16)],
            [place, line_first, raw],
            "near",
            [False, False, True],
            tile,
            [True],
            flops=2 * height * tokens * width,
        )[0]
        return flip(payload, SEATS)

    def relay(line, far):
        payload = call(
            bind(relay_kernel, cap),
            [((2 * height, width), BF16)],
            [place, line, *far],
            "relay",
            [False, False, True, True],
            tile,
            [True],
            flops=4 * height * tokens * width,
        )[0]
        return send(payload, OUTWARD)

    def spread(line, raw, near, far, passed):
        blocks = call(
            bind(spread_kernel, cap),
            [((height, width), BF16)] * SEATS,
            [place, line, raw, near, *far, passed],
            "spread",
            [False, False] + [True] * 5,
            tile,
            [True] * SEATS,
            [
                pltpu.VMEM((rows, tokens), BF16),
                pltpu.VMEM((rows, height), BF16),
                pltpu.VMEM((rows, tokens), BF16),
                pltpu.VMEM((rows, tokens), BF16),
                pltpu.VMEM((rows, 2 * height), BF16),
                pltpu.VMEM((rows, 128), F32),
            ],
            flops=2 * rows * (3 * tokens + 3 * height) * width,
        )
        return [blocks[0]] + [flip(blocks[j], j) for j in range(1, SEATS)]

    def expert(turned, arrived):
        return call(
            bind(expert_kernel, cap),
            [((rows, depth), BF16), ((experts, 128), F32)],
            [place, weight, turned, *arrived],
            "expert",
            [False, True, False] + [True] * SEATS,
            tile,
            None,
            [pltpu.VMEM((rows, depth), F32)],
            flops=2 * rows * depth * width,
        )

    def sorted_rows(blocks):
        near, passed = call(
            bind(sort_kernel, cap),
            [((height, width), BF16), ((2 * height, width), BF16)],
            blocks,
            "sort",
            [True] * SEATS,
            tile,
            [True, True],
            flops=6 * height * rows * width,
        )
        return flip(near, SEATS), send(passed, INWARD)

    def merged(line, blocks, passed):
        to_a, to_b = call(
            bind(merge_kernel, cap),
            [((tokens, width), BF16)] * 2,
            [place, line, *blocks, passed],
            "merge",
            [False, False] + [True] * (SEATS + 1),
            tile,
            [True, True],
            flops=8 * tokens * (rows + 2 * height) * width,
        )
        return send(to_a, BACK_A), send(to_b, BACK_B)

    blocks_own = outputs(turned_own)
    near_own = near_rows(table, raw_own)
    blocks_other = outputs(turned_other)
    far_other = send(raw_other, FAR_A), send(raw_other, FAR_B)
    near_other = near_rows(line_other[0], raw_other)
    back_near_other, back_passed_other = sorted_rows(blocks_other)
    passed_own = relay(line_own, far_own)
    back_near_own, back_passed_own = sorted_rows(blocks_own)
    dense_other = merged(line_other, blocks_other, back_passed_other)
    arrived_own = spread(line_own, raw_own, near_own, far_own, passed_own)
    dense_own = merged(line_own, blocks_own, back_passed_own)
    passed_other = relay(line_other, far_other)
    partial_own, scores_own = expert(turned_own, arrived_own)
    arrived_other = spread(line_other, raw_other, near_other, far_other, passed_other)
    mixed_other = call(
        bind(other_tokens_kernel, cap),
        [((tokens, width), BF16)],
        [place, line_other, *blocks_other, back_near_other, *dense_other],
        "tokens_other",
        [False, False] + [True] * (SEATS + 3),
        tile,
        [True],
        flops=4 * tokens * (rows + height) * width,
    )[0]
    crossed = swap(mixed_other)
    partial_other, scores_other = expert(turned_other, arrived_other)
    partial_crossed = swap(partial_other)
    scores = scores_own + swap(scores_other)
    scores = lax.all_to_all(scores, "exp", split_axis=0, concat_axis=0, tiled=True)
    weight_grad = call(
        weight_kernel,
        [((depth, 2 * width // 2), BF16)],
        [turned_own, turned_other, *arrived_own, *arrived_other],
        "weight_grad",
        [False, False] + [True] * (2 * SEATS),
        tile,
        [True],
        flops=4 * rows * depth * width,
    )[0]
    hidden_grad = call(
        bind(hidden_kernel, cap),
        [((rows, depth), BF16)],
        [place, partial_own, partial_crossed],
        "hidden_grad",
    )[0]
    combined, gate_grad = call(
        bind(own_tokens_kernel, cap),
        [((tokens, 2 * width), BF16), ((2, tokens), F32)],
        [place, line_own, ids, scores, crossed, *blocks_own, back_near_own, *dense_own],
        "tokens_own",
        flops=4 * tokens * (rows + height) * width,
    )
    return (combined, hidden_grad[None, None], weight_grad[None], gate_grad.T)


def solution(mesh):
    small = mesh.shape["rep"] == 2 and mesh.shape["exp"] == PLANES * SEATS
    return jax.shard_map(
        planes_and_seats if small else general,
        mesh=mesh,
        in_specs=(
            P("rep", "exp", None, None),
            P("exp", None, "rep"),
            P(("rep", "exp"), None),
            P(("rep", "exp"), None),
            P(("rep", "exp"), None),
        ),
        out_specs=(
            P(("rep", "exp"), None),
            P("rep", "exp", None, None),
            P("exp", None, "rep"),
            P(("rep", "exp"), None),
        ),
        check_vma=False,
    )
```

```python
import functools

import jax
import jax.numpy as jnp
from jax import lax
from jax.experimental import pallas as pl
from jax.experimental.pallas import tpu as pltpu
from jax.sharding import PartitionSpec as P


PLANES = 4
SEATS = 4
BF16 = jnp.bfloat16
F32 = jnp.float32


def slot_tables(routed, gate_weights, expert_count, capacity):
    token_count = routed.shape[0]
    matches = (routed[:, :, None] == jnp.arange(expert_count, dtype=jnp.int32)).astype(jnp.int32)
    per_token = jnp.sum(matches, axis=1)
    before = jnp.cumsum(per_token, axis=0) - per_token
    position = jnp.sum(matches * before[:, None, :], axis=2)
    target = routed * capacity + position
    matched = target[:, :, None] == jnp.arange(expert_count * capacity, dtype=jnp.int32)
    token_index = jnp.arange(token_count, dtype=jnp.int32)[:, None, None]
    slot_token = jnp.sum(jnp.where(matched, token_index, 0), axis=(0, 1))
    slot_gate = jnp.sum(jnp.where(matched, gate_weights[:, :, None], 0.0), axis=(0, 1))
    return (target, slot_token, slot_gate)


def general(hidden, down_weight, grad_out, expert_ids, gate_weights):
    rep_count = lax.axis_size("rep")
    exp_count = lax.axis_size("exp")
    slots_all = hidden.shape[2]
    capacity = slots_all // exp_count
    token_count, model_width = grad_out.shape
    top_count = expert_ids.shape[1]
    slice_width = model_width // rep_count
    target, slot_token, slot_gate = slot_tables(expert_ids, gate_weights, exp_count, capacity)
    weights_local = down_weight[0]
    grad_split = (
        grad_out.reshape(token_count, rep_count, slice_width).transpose(1, 0, 2).astype(F32)
    )
    outgoing = (jnp.take(grad_split, slot_token, axis=1) * slot_gate[None, :, None]).astype(BF16)
    outgoing = outgoing.reshape(rep_count, exp_count, capacity, slice_width)
    arrived = lax.all_to_all(
        lax.all_to_all(outgoing, "exp", split_axis=1, concat_axis=1, tiled=True),
        "rep",
        split_axis=0,
        concat_axis=0,
        tiled=True,
    )
    arrived = arrived.reshape(rep_count, slots_all, slice_width)
    gathered = lax.all_gather(hidden[0], "rep", axis=0, tiled=True)
    outputs = jnp.einsum(
        "rnf,fd->rnd", gathered, weights_local, preferred_element_type=F32
    ).astype(BF16)
    outputs = outputs.reshape(rep_count, exp_count, capacity, slice_width)
    returned = lax.all_to_all(
        lax.all_to_all(outputs, "exp", split_axis=1, concat_axis=1, tiled=True),
        "rep",
        split_axis=0,
        concat_axis=0,
        tiled=True,
    )
    returned = returned.reshape(rep_count, exp_count * capacity, slice_width)
    weight_grad = jnp.einsum(
        "rnf,rnd->fd", gathered, arrived, preferred_element_type=F32
    ).astype(BF16)[None]
    hidden_sum = lax.psum_scatter(
        jnp.einsum(
            "rnd,fd->rnf", arrived, weights_local, preferred_element_type=F32
        ).astype(BF16),
        "rep",
        scatter_dimension=0,
        tiled=True,
    )
    picked = jnp.take(returned, target.reshape(-1), axis=1)
    picked = picked.reshape(rep_count, token_count, top_count, slice_width).transpose(1, 2, 0, 3)
    picked = picked.reshape(token_count, top_count, model_width).astype(F32)
    combined = jnp.sum(gate_weights[:, :, None] * picked, axis=1).astype(BF16)
    gate_grad = jnp.sum(grad_out.astype(F32)[:, None, :] * picked, axis=2)
    return (combined, hidden_sum[None], weight_grad, gate_grad)


def part(index, unit, count):
    return sum([(index >= unit * i).astype(jnp.int32) for i in range(1, count)])


def axes(shape, dim, capacity):
    row = lax.broadcasted_iota(jnp.int32, shape, dim)
    width = PLANES * capacity
    j = part(row, width, SEATS)
    rest = row - j * width
    g = part(rest, capacity, PLANES)
    return j, g, rest - g * capacity


def hot(mask):
    return jnp.where(mask, 1.0, 0.0).astype(BF16)


def names(table, wanted):
    wanted = wanted.astype(F32)
    return wanted == table[0:1, :], wanted == table[1:2, :]


def mm(a, b):
    return jnp.dot(a, b, preferred_element_type=F32)


def mm_tn(a, b):
    return lax.dot_general(a, b, (((0,), (0,)), ((), ())), preferred_element_type=F32)


def mm_nt(a, b):
    return lax.dot_general(a, b, (((1,), (1,)), ((), ())), preferred_element_type=F32)


def start_kernel(cap, ids, gates, table):
    experts, tokens = PLANES * SEATS, ids.shape[1]
    expert = lax.broadcasted_iota(jnp.int32, (experts, tokens), 0)
    first, second = expert == ids[0:1, :], expert == ids[1:2, :]
    earlier = lax.broadcasted_iota(jnp.int32, (tokens, tokens), 0) < lax.broadcasted_iota(
        jnp.int32, (tokens, tokens), 1
    )
    before = mm(hot(first | second), hot(earlier))
    slot = expert.astype(F32) * cap + before
    table[...] = jnp.zeros_like(table)
    table[0:1, :] = jnp.sum(jnp.where(first, slot, 0.0), axis=0, keepdims=True)
    table[1:2, :] = jnp.sum(jnp.where(second, slot, 0.0), axis=0, keepdims=True)
    table[2:4, :] = gates[...]


def turn_matrix(place, rows, cap):
    j, g, slot = axes((rows, rows), 0, cap)
    column = lax.broadcasted_iota(jnp.int32, (rows, rows), 1)
    return hot(column == ((place[0] ^ g) * SEATS + (place[1] ^ j)) * cap + slot)


def project_kernel(cap, place, hidden, weight, turned, *outs):
    @pl.when(pl.program_id(0) == 0)
    def _():
        turned[...] = mm(turn_matrix(place, hidden.shape[0], cap), hidden[...]).astype(BF16)

    full = mm(turned[...], weight[...]).astype(BF16)
    height = outs[0].shape[0]
    for j, out in enumerate(outs):
        out[...] = full[j * height : (j + 1) * height, :]


def near_kernel(place, table, raw, out):
    rows, tokens = out.shape[0], raw.shape[0]
    wanted = (place[0] ^ 1) * rows + lax.broadcasted_iota(jnp.int32, (rows, tokens), 0)
    first, second = names(table[...], wanted)
    out[...] = mm(hot(first | second), raw[...]).astype(BF16)


def relay_rows(place, line, far_a, far_b, out):
    rows, tokens = out.shape[0] // 2, far_a.shape[0]
    wanted = (place[0] ^ 1) * rows + lax.broadcasted_iota(jnp.int32, (rows, tokens), 0)
    for half, (table, far) in enumerate(((line[3], far_b), (line[2], far_a))):
        first, second = names(table, wanted)
        out[half * rows : (half + 1) * rows, :] = mm(hot(first | second), far[...]).astype(BF16)


def relay_own_kernel(place, t0, t1, t2, t3, far_a, far_b, out, line):
    tables = (t0[...], t1[...], t2[...], t3[...])
    for g, table in enumerate(tables):
        line[g] = table
    relay_rows(place, tables, far_a, far_b, out)


def relay_other_kernel(place, line, far_a, far_b, out):
    relay_rows(place, line, far_a, far_b, out)


def spread_kernel(cap, place, line, raw, near, far_a, far_b, passed, *rest):
    outs, (direct, m_passed, scale) = rest[:SEATS], rest[SEATS:]
    height, tokens = outs[0].shape[0], raw.shape[0]
    rows = SEATS * height

    @pl.when(pl.program_id(0) == 0)
    def _():
        j, g, slot = axes((rows, tokens), 0, cap)
        wanted = place[0] * height + (place[1] ^ j) * cap + slot
        total = jnp.zeros((rows, tokens), F32)
        for group, column in ((0, 0), (1, None), (2, 1), (3, 2)):
            first, second = names(line[group], wanted)
            first, second = first & (g == group), second & (g == group)
            if column is not None:
                direct[:, column * tokens : (column + 1) * tokens] = hot(first | second)
            total += jnp.where(first, line[group][2:3, :], 0.0)
            total += jnp.where(second, line[group][3:4, :], 0.0)
        scale[...] = jnp.broadcast_to(jnp.sum(total, axis=1, keepdims=True), scale.shape)
        j, g, slot = axes((rows, height), 0, cap)
        column = lax.broadcasted_iota(jnp.int32, (rows, height), 1)
        direct[:, 3 * tokens :] = hot((g == 1) & (column == (place[1] ^ j) * cap + slot))
        j, g, slot = axes((rows, 2 * height), 0, cap)
        column = lax.broadcasted_iota(jnp.int32, (rows, 2 * height), 1)
        m_passed[...] = hot((g >= 2) & (column == (g - 2) * height + (place[1] ^ j) * cap + slot))

    def store(full):
        full = (full * scale[:, 0:1]).astype(BF16)
        for j, out in enumerate(outs):
            out[...] = full[j * height : (j + 1) * height, :]

    middle = (place[0] == 1) | (place[0] == 2)

    @pl.when(middle)
    def _():
        store(
            mm(direct[:, : 2 * tokens], jnp.concatenate([raw[...], far_a[...]], axis=0))
            + mm(direct[:, 2 * tokens :], jnp.concatenate([far_b[...], near[...]], axis=0))
        )

    @pl.when(jnp.logical_not(middle))
    def _():
        store(
            mm(direct[:, :tokens], raw[...])
            + mm(direct[:, 3 * tokens :], near[...])
            + mm(m_passed[...], passed[...])
        )


def expert_kernel(cap, place, weight, turned, a0, a1, a2, a3, partial, scores, total):
    arrived = jnp.concatenate([a0[...], a1[...], a2[...], a3[...]], axis=0)
    step = pl.program_id(0)

    @pl.when(step == 0)
    def _():
        total[...] = jnp.zeros_like(total)

    total[...] += mm_nt(arrived, weight[...])

    @pl.when(step == pl.num_programs(0) - 1)
    def _():
        whole = total[...]
        partial[...] = whole.astype(BF16)
        score = jnp.sum(whole * turned[...].astype(F32), axis=1, keepdims=True)
        rows, lanes = whole.shape[0], scores.shape[1]
        j, g, slot = axes((rows, lanes), 0, cap)
        column = lax.broadcasted_iota(jnp.int32, (rows, lanes), 1)
        spread = jnp.where(column == slot, score, 0.0)
        sources = scores.shape[0]
        j, g, slot = axes((sources, rows), 1, cap)
        source = lax.broadcasted_iota(jnp.int32, (sources, rows), 0)
        pick = jnp.where(source == (place[0] ^ g) * SEATS + (place[1] ^ j), 1.0, 0.0)
        scores[...] = jnp.dot(
            pick, spread, preferred_element_type=F32, precision=lax.Precision.HIGHEST
        )


def weight_kernel(own_turned, other_turned, *rest):
    arrived, out, turned = rest[: 2 * SEATS], rest[2 * SEATS], rest[2 * SEATS + 1]

    @pl.when(pl.program_id(0) == 0)
    def _():
        turned[...] = jnp.concatenate([own_turned[...], other_turned[...]], axis=0).T

    full = jnp.concatenate([r[...] for r in arrived], axis=0)
    out[...] = mm(turned[...], full).astype(BF16)


def hidden_kernel(cap, place, mine, theirs, out):
    total = (mine[...].astype(F32) + theirs[...].astype(F32)).astype(BF16)
    out[...] = mm_tn(turn_matrix(place, total.shape[0], cap), total).astype(BF16)


def sort_kernel(cap, q0, q1, q2, q3, *outs):
    full = jnp.concatenate([q0[...], q1[...], q2[...], q3[...]], axis=0)
    height, rows = outs[0].shape[0], full.shape[0]
    j, g, slot = axes((rows, rows), 1, cap)
    row = lax.broadcasted_iota(jnp.int32, (rows, rows), 0)
    out_rows = mm(hot(row == g * height + j * cap + slot), full).astype(BF16)
    for g, out in enumerate(outs):
        out[...] = out_rows[g * height : (g + 1) * height, :]


def gather_weights(cap, place, table, rows):
    tokens = table.shape[1]
    columns = table.T
    row = lax.broadcasted_iota(jnp.int32, (tokens, rows), 1)
    height = SEATS * cap
    g = part(row, height, PLANES)
    rest = row - g * height
    j = part(rest, cap, SEATS)
    wanted = (place[0] ^ g) * height + (place[1] ^ j) * cap + rest - j * cap
    wanted = wanted.astype(F32)
    gates = jnp.where(wanted == columns[:, 0:1], columns[:, 2:3], 0.0)
    gates += jnp.where(wanted == columns[:, 1:2], columns[:, 3:4], 0.0)
    hi = gates.astype(BF16)
    return jnp.concatenate([hi, (gates - hi.astype(F32)).astype(BF16)], axis=0)


def token_rows(weights, blocks):
    home, near, *far = [r[...] for r in blocks]
    both = mm(weights, jnp.concatenate([home, near, far[0] + far[1], far[2] + far[3]], axis=0))
    tokens = both.shape[0] // 2
    return (both[:tokens, :] + both[tokens:, :]).astype(BF16)


def other_tokens_kernel(cap, place, table, b0, b1, b2, b3, b4, b5, out, weights):
    @pl.when(pl.program_id(0) == 0)
    def _():
        weights[...] = gather_weights(cap, place, table[...], weights.shape[1])

    out[...] = token_rows(weights[...], (b0, b1, b2, b3, b4, b5))


def own_tokens_kernel(cap, place, table, ids, scores, crossed, *rest):
    *blocks, out, gate_grad = rest
    b0 = blocks[0]
    width = crossed.shape[1]
    rows = PLANES * b0.shape[0]
    weights = gather_weights(cap, place, table[...], rows)
    out[:, pl.ds(pl.multiple_of((1 - place[2]) * width, width), width)] = crossed[...]
    mine = token_rows(weights, blocks)
    out[:, pl.ds(pl.multiple_of(place[2] * width, width), width)] = mine
    sources, lanes = scores.shape
    tokens = mine.shape[0]
    expert = lax.broadcasted_iota(jnp.int32, (sources, tokens), 0)
    lane = lax.broadcasted_iota(jnp.int32, (lanes, tokens), 0).astype(F32)
    for k in range(2):
        name = ids[k : k + 1, :]
        chosen = jnp.where(expert == name, 1.0, 0.0)
        spread = lax.dot_general(
            scores[...],
            chosen,
            (((0,), (0,)), ((), ())),
            preferred_element_type=F32,
            precision=lax.Precision.HIGHEST,
        )
        position = table[k : k + 1, :] - name.astype(F32) * cap
        score = jnp.sum(jnp.where(lane == position, spread, 0.0), axis=0, keepdims=True)
        gate_grad[k : k + 1, :] = score / table[2 + k : 3 + k, :]


SMEM = pl.BlockSpec(memory_space=pltpu.SMEM)


def call(kernel, outs, args, name, blocked=None, tile=None, out_blocked=None, scratch=(), flops=0):
    shapes = [jax.ShapeDtypeStruct(s, d) for s, d in outs]
    moved = sum(a.size * a.dtype.itemsize for a in args) + sum(
        s.size * s.dtype.itemsize for s in shapes
    )
    blocked = blocked or [False] * len(args)
    out_blocked = out_blocked or [False] * len(outs)

    def spec(shape, cut):
        if cut:
            return pl.BlockSpec((shape[0], tile), lambda i: (0, i))
        return pl.BlockSpec(shape, lambda *i: (0,) * len(shape))

    grid = ()
    if tile:
        width = next(a.shape[1] for a, cut in zip(args, blocked) if cut)
        grid = (width // tile,)
    in_specs = [
        SMEM if (a.ndim == 1 and a.dtype == jnp.int32) else spec(a.shape, cut)
        for a, cut in zip(args, blocked)
    ]
    return pl.pallas_call(
        kernel,
        out_shape=shapes,
        grid=grid,
        in_specs=in_specs,
        out_specs=[spec(s.shape, cut) for s, cut in zip(shapes, out_blocked)],
        scratch_shapes=list(scratch),
        compiler_params=pltpu.CompilerParams(vmem_limit_bytes=(63 if name == "k_weight" else 32) << 20),
        cost_estimate=pl.CostEstimate(flops=int(flops), bytes_accessed=int(moved), transcendentals=0),
    )(*args)


def over_planes(moves):
    return [
        (a * SEATS + seat, b * SEATS + seat) for a, b in moves for seat in range(SEATS)
    ]


FAR_A = over_planes([(0, 2), (3, 1)])
FAR_B = over_planes([(1, 2), (2, 1)])
OUTWARD = over_planes([(2, 3), (1, 0)])
BACK_A = over_planes([(2, 0), (1, 3)])
ACROSS = over_planes([(0, 3), (3, 0)])


def send(x, pairs):
    return lax.ppermute(x, "exp", pairs)


def swap(x):
    return lax.ppermute(x, "rep", [(0, 1), (1, 0)])


def flip(x, bits):
    return send(x, [(s, s ^ bits) for s in range(PLANES * SEATS)])


def planes_and_seats(hidden, down_weight, grad_out, expert_ids, gate_weights):
    return steps(hidden, down_weight, grad_out, expert_ids, gate_weights)


def steps(hidden, down_weight, grad_out, expert_ids, gate_weights):
    replica, device = lax.axis_index("rep"), lax.axis_index("exp")
    place = jnp.stack([device // SEATS, device % SEATS, replica]).astype(jnp.int32)
    rows, depth = hidden.shape[2:]
    experts = PLANES * SEATS
    cap = rows // experts
    height = PLANES * cap
    tokens, width = grad_out.shape[0], grad_out.shape[1] // 2
    weight = down_weight[0]
    tile = width // 2 if width % 512 == 0 else width
    ids, gates = expert_ids.T, gate_weights.T
    bind = functools.partial

    def spread_out(blocks):
        return [blocks[0]] + [flip(blocks[j], j) for j in range(1, SEATS)]

    def far(raw):
        return send(raw, FAR_A), send(raw, FAR_B)

    def near(who, table, raw):
        payload = call(
            near_kernel,
            [((height, width), BF16)],
            [place, table, raw],
            "k_near_" + who,
            [False, False, True],
            tile,
            [True],
            flops=2 * height * tokens * width,
        )[0]
        return flip(payload, SEATS)

    def project(who, hidden_rows):
        turned, *blocks = call(
            bind(project_kernel, cap),
            [((rows, depth), BF16)] + [((height, width), BF16)] * SEATS,
            [place, hidden_rows, weight],
            "k_project_" + who,
            [False, False, True],
            tile,
            [False] + [True] * SEATS,
            flops=2 * rows * depth * width,
        )
        return turned, spread_out(blocks)

    def relay(who, kernel, tables, far_rows, more=()):
        payload, *rest = call(
            kernel,
            [((2 * height, width), BF16), *more],
            [place, *tables, *far_rows],
            "k_relay_" + who,
            [False] * (1 + len(tables)) + [True, True],
            tile,
            [True] + [False] * len(more),
            flops=4 * height * tokens * width,
        )
        return send(payload, OUTWARD), *rest

    def spread(who, line, raw, near_rows, far_rows, passed):
        blocks = call(
            bind(spread_kernel, cap),
            [((height, width), BF16)] * SEATS,
            [place, line, raw, near_rows, *far_rows, passed],
            "k_spread_" + who,
            [False, False] + [True] * 5,
            tile,
            [True] * SEATS,
            [
                pltpu.VMEM((rows, 3 * tokens + height), BF16),
                pltpu.VMEM((rows, 2 * height), BF16),
                pltpu.VMEM((rows, 128), F32),
            ],
            flops=2 * rows * (3 * tokens + 3 * height) * width,
        )
        return spread_out(blocks)

    def expert(who, turned, arrived):
        return call(
            bind(expert_kernel, cap),
            [((rows, depth), BF16), ((experts, 128), F32)],
            [place, weight, turned, *arrived],
            "k_expert_" + who,
            [False, True, False] + [True] * SEATS,
            tile,
            None,
            [pltpu.VMEM((rows, depth), F32)],
            flops=2 * rows * depth * width,
        )

    def sort(who, blocks):
        by_plane = call(
            bind(sort_kernel, cap),
            [((height, width), BF16)] * PLANES,
            blocks,
            "k_sort_" + who,
            [True] * SEATS,
            tile,
            [True] * PLANES,
            flops=2 * rows * rows * width,
        )
        near_rows = flip(by_plane[1], SEATS)
        far_rows = [
            send(by_plane[g], pairs)
            for g, pairs in ((2, FAR_A), (2, BACK_A), (3, FAR_B), (3, ACROSS))
        ]
        return [by_plane[0], near_rows, *far_rows]

    hidden_x = swap(hidden[0, 0])
    raw_leaving = lax.dynamic_slice_in_dim(grad_out, (1 - replica) * width, width, axis=1)
    raw_o = lax.dynamic_slice_in_dim(grad_out, replica * width, width, axis=1)
    raw_x = swap(raw_leaving)
    far_o = far(raw_o)
    table = call(bind(start_kernel, cap), [((8, tokens), F32)], [ids, gates], "k_tables")[0]
    turned_x, blocks_x = project("x", hidden_x)
    turned_o, blocks_o = project("o", hidden[0, 0])
    near_o = near("o", table, raw_o)
    tables = [table] + [flip(table, g * SEATS) for g in range(1, PLANES)]
    far_x = far(raw_x)
    passed_o, line_o = relay(
        "o", relay_own_kernel, tables, far_o, [((PLANES, *table.shape), F32)]
    )
    line_x = swap(line_o)
    home_x = sort("x", blocks_x)
    home_o = sort("o", blocks_o)
    near_x = near("x", line_x[0], raw_x)
    arrived_o = spread("o", line_o, raw_o, near_o, far_o, passed_o)
    passed_x = relay("x", relay_other_kernel, [line_x], far_x)[0]
    partial_o, scores_o = expert("o", turned_o, arrived_o)
    arrived_x = spread("x", line_x, raw_x, near_x, far_x, passed_x)
    mixed_x = call(
        bind(other_tokens_kernel, cap),
        [((tokens, width), BF16)],
        [place, line_x[0], *home_x],
        "k_tokens_x",
        [False, False] + [True] * len(home_x),
        tile,
        [True],
        [pltpu.VMEM((2 * tokens, rows), BF16)],
        flops=4 * tokens * rows * width,
    )[0]
    crossed = swap(mixed_x)
    partial_x, scores_x = expert("x", turned_x, arrived_x)
    scores = scores_o + swap(scores_x)
    partial_crossed = swap(partial_x)
    scores = lax.all_to_all(scores, "exp", split_axis=0, concat_axis=0, tiled=True)
    weight_grad = call(
        weight_kernel,
        [((depth, width), BF16)],
        [turned_o, turned_x, *arrived_o, *arrived_x],
        "k_weight",
        [False, False] + [True] * (2 * SEATS),
        tile,
        [True],
        [pltpu.VMEM((depth, 2 * rows), BF16)],
        flops=4 * rows * depth * width,
    )[0]
    hidden_grad = call(
        bind(hidden_kernel, cap),
        [((rows, depth), BF16)],
        [place, partial_o, partial_crossed],
        "k_hidden",
    )[0]
    combined, gate_grad = call(
        bind(own_tokens_kernel, cap),
        [((tokens, 2 * width), BF16), ((2, tokens), F32)],
        [place, table, ids, scores, crossed, *home_o],
        "k_tokens_o",
        flops=4 * tokens * rows * width,
    )
    return (combined, hidden_grad[None, None], weight_grad[None], gate_grad.T)


def solution(mesh):
    small = mesh.shape["rep"] == 2 and mesh.shape["exp"] == PLANES * SEATS
    return jax.shard_map(
        planes_and_seats if small else general,
        mesh=mesh,
        in_specs=(
            P("rep", "exp", None, None),
            P("exp", None, "rep"),
            P(("rep", "exp"), None),
            P(("rep", "exp"), None),
            P(("rep", "exp"), None),
        ),
        out_specs=(
            P(("rep", "exp"), None),
            P("rep", "exp", None, None),
            P("exp", None, "rep"),
            P(("rep", "exp"), None),
        ),
        check_vma=False,
    )
```
